32 devices in a mesh: group: 2 (over x), cell: 16 (over z, y, core).
Axes of the slice: x: 2, y: 2, z: 4, core: 2. Of those that a mesh axis runs over, the one named last changes fastest.
Arguments:
- cell_factor: bfloat16 [32768, 128], P(('group', 'cell')), parts along dimension 0, may hold values from -6 to 6
- sched_factor: bfloat16 [16384, 128], P('group'), parts along dimension 0, may hold values from -6 to 6
- core_matrix: float32 [256, 128], P('group'), parts along dimension 0, may hold values from -0.03125 to 0.03125
- rate_table: bfloat16 [64, 128], replicated, may hold values from 0.5 to 2
- cell_well: int32 [32768], P(('group', 'cell')), parts along dimension 0, may hold values from 0 to 63
- sched_profile: int32 [16384], P('group'), parts along dimension 0, may hold values from 0 to 127
Outputs:
- basis_cells: float32 [32768, 256], P(('group', 'cell')), parts along dimension 0
- basis_sched: float32 [16384, 256], P(('group', 'cell')), parts along dimension 0
- core_out: float32 [512, 256], P('group'), parts along dimension 0
The draws below stay inside these ranges and needn't reach their ends.
There are 2 independent parts, one for each index of `group`. The reference program is written for one: setup_inputs(seed, part) draws one part's arguments, and reference() takes and returns one part's arrays. A program takes and returns all parts, laid end to end along the dimension named above; an argument that names none is the same for every part. Nothing has to cross between parts.
All inputs are finite; a program needn't handle non-finite values.
Results may differ from the reference program's by a relative error of at most 0.02.
Values may be sent and summed in bfloat16 or wider, within the bound.
A program may use at most 128 MiB of HBM per device.

```python
import jax
import jax.numpy as jnp
from jax import lax

R = 128
P_SIZE = 128
W = 64
CELL_DEV = 1024
NS = 8192
NC = 16384


def plant(entries, own_key, least, top_value):
    longest = entries.shape.index(max(entries.shape))
    spots = []
    for shift in (0, 1):
        where = [jax.random.randint(jax.random.fold_in(own_key, axis), (), 0, length) for axis, length in enumerate(entries.shape)]
        where[longest] = (where[longest] + shift) % entries.shape[longest]
        spots.append(tuple(where))
    return entries.at[spots[0]].set(least).at[spots[1]].set(top_value)


def shard_levels(rng, dims, split, smallest, high):
    level = 1.0
    for position, shards_of in split:
        steps = jax.random.uniform(jax.random.fold_in(jax.random.fold_in(rng, 6), position), (shards_of,), jnp.float32, smallest / len(split), high / len(split))
        level = level * jnp.repeat(jnp.exp(steps), dims[position] // shards_of).reshape((-1,) + (1,) * (len(dims) - 1 - position))
    return level


def noise(rng, dims, width, bound, split=(), held_as=jnp.bfloat16):
    values = width * jax.random.normal(rng, dims, jnp.float32)
    if split:
        values = values * shard_levels(rng, dims, split, -0.22, 0.18)
    return jnp.clip(values, -bound, bound).astype(held_as)


def setup_inputs(seed: int = 0, part: int = 0) -> dict:
    seeds = jax.random.split(jax.random.key(seed), 7)
    part_splits = jax.random.split(jax.random.fold_in(seeds[6], part), 7)
    return {
        "cell_factor": noise(part_splits[0], (NC, R), 1.0, 6.0, ((0, 16),)),
        "sched_factor": noise(part_splits[1], (NS, R), 1.0, 6.0),
        "core_matrix": noise(part_splits[2], (R, R), (1.0 / R), 0.03125, (), jnp.float32),
        "rate_table": jnp.clip(jax.random.uniform(seeds[3], (W, P_SIZE), jnp.float32, 0.5, 2.0), 0.5, 2.0).astype(jnp.bfloat16),
        "cell_well": plant(jax.random.randint(part_splits[4], (NC,), 0, W), jax.random.fold_in(part_splits[4], 1), 0, W - 1).astype(jnp.int32),
        "sched_profile": plant(jax.random.randint(part_splits[5], (NS,), 0, P_SIZE), jax.random.fold_in(part_splits[5], 1), 0, P_SIZE - 1).astype(jnp.int32),
    }


TIME_STEP = 0.25
PANEL_SCALE = 8.0

def local_gram(panel):
    return lax.dot_general(panel, panel, (((0,), (0,)), ((), ())), precision=lax.Precision.HIGHEST)

def orth_step(panel, gram):
    factor_low = jnp.linalg.cholesky(gram)
    return lax.linalg.triangular_solve(factor_low, panel, left_side=False, lower=True, transpose_a=True)

def orthonormal(panel):
    return orth_step(panel, local_gram(panel))

def build_tile(cell_rows, cell_wells, sched_factor, core_matrix, rate_table, prof_onehot):
    factor_mix = jnp.dot(cell_rows.astype(jnp.float32), core_matrix, precision=lax.Precision.HIGHEST).astype(jnp.bfloat16)
    rebuilt = lax.dot_general(factor_mix.astype(jnp.float32), sched_factor.astype(jnp.float32), (((1,), (1,)), ((), ())), preferred_element_type=jnp.float32)
    cell_rates = rate_table[cell_wells]
    inject = lax.dot_general(cell_rates.astype(jnp.float32), prof_onehot.astype(jnp.float32), (((1,), (1,)), ((), ())), preferred_element_type=jnp.float32)
    return (rebuilt + TIME_STEP * (rebuilt - rebuilt * rebuilt * rebuilt + inject)).astype(jnp.bfloat16)

def reference(cell_factor, sched_factor, core_matrix, rate_table, cell_well, sched_profile):
    n_cells = cell_factor.shape[0]
    n_sched = sched_factor.shape[0]
    widths = cell_factor.shape[1]
    blocks = n_cells // CELL_DEV
    profiles = rate_table.shape[1]
    prof_onehot = (sched_profile[:, None] == jnp.arange(profiles, dtype=jnp.int32)[None, :]).astype(jnp.bfloat16)
    factor_blocks = cell_factor.reshape(blocks, CELL_DEV, widths)
    well_blocks = cell_well.reshape(blocks, CELL_DEV)

    def first(carry, inputs):
        cell_rows, cell_wells = inputs
        tile_state = build_tile(cell_rows, cell_wells, sched_factor, core_matrix, rate_table, prof_onehot)
        k_part = jnp.dot(tile_state.astype(jnp.float32), sched_factor.astype(jnp.float32), preferred_element_type=jnp.float32)
        l_part = lax.dot_general(tile_state.astype(jnp.float32), cell_rows.astype(jnp.float32), (((0,), (0,)), ((), ())), preferred_element_type=jnp.float32)
        return (carry + l_part, k_part)
    l_proj, k_parts = lax.scan(first, jnp.zeros((n_sched, widths), jnp.float32), (factor_blocks, well_blocks))
    k_proj = k_parts.reshape(n_cells, widths)
    panel_u = jnp.concatenate([cell_factor.astype(jnp.float32), k_proj * (PANEL_SCALE / n_sched)], axis=1)
    panel_v = jnp.concatenate([sched_factor.astype(jnp.float32), l_proj * (PANEL_SCALE / n_cells)], axis=1)
    basis_u = orthonormal(panel_u)
    basis_v = orthonormal(panel_v)
    basis_low = basis_v.astype(jnp.bfloat16)
    basis_blocks = basis_u.reshape(blocks, CELL_DEV, 2 * widths)

    def second(carry, inputs):
        cell_rows, cell_wells, basis_rows = inputs
        tile_state = build_tile(cell_rows, cell_wells, sched_factor, core_matrix, rate_table, prof_onehot)
        galerkin = jnp.dot(tile_state.astype(jnp.float32), basis_low.astype(jnp.float32), preferred_element_type=jnp.float32)
        term = lax.dot_general(basis_rows, galerkin, (((0,), (0,)), ((), ())), precision=lax.Precision.HIGHEST)
        return (carry + term, 0)
    core_sum, unused = lax.scan(second, jnp.zeros((2 * widths, 2 * widths), jnp.float32), (factor_blocks, well_blocks, basis_blocks))
    basis_cells = basis_u * jnp.sqrt(jnp.float32(n_cells))
    basis_sched = basis_v * jnp.sqrt(jnp.float32(n_sched))
    core_out = core_sum * (widths / jnp.sqrt(jnp.float32(n_cells) * jnp.float32(n_sched)))
    return (basis_cells, basis_sched, core_out)
```

```python
import functools

import jax
import jax.numpy as jnp
from jax import lax
from jax.experimental import pallas as pl
from jax.experimental.pallas import tpu as pltpu
from jax.sharding import PartitionSpec as P

TIME_STEP = 0.25
PANEL_SCALE = 8.0
HIGH = lax.Precision.HIGHEST
F32 = jnp.float32
BF16 = jnp.bfloat16
CHUNKS = 8
BLOCK = 16
VMEM_LIMIT = 48 * 1000 * 1000
HAND_LIMIT = 16 * 1000 * 1000


def dot(a, b, ca, cb, precision=None):
    return lax.dot_general(
        a, b, (((ca,), (cb,)), ((), ())), precision=precision, preferred_element_type=F32
    )


def eliminate(ws, low, high):
    n = ws[0].shape[0]
    lane = lax.broadcasted_iota(jnp.int32, (1, n), 1)
    rid = lax.broadcasted_iota(jnp.int32, (BLOCK, 1), 0)

    def body(b, carry):
        base = pl.multiple_of(b * BLOCK, BLOCK)
        rows = [w[pl.ds(base, BLOCK), :] for w in ws]
        cols = [
            [
                jnp.sum(jnp.where(lane == base + t, r[:, 0:n], 0.0), axis=1, keepdims=True)
                for t in range(BLOCK)
            ]
            for r in rows
        ]
        inverse = [jnp.zeros((BLOCK, 1), F32) for _ in ws]
        for t in range(BLOCK):
            for m in range(len(ws)):
                col = cols[m]
                recip = 1.0 / col[t][t : t + 1, :]
                inverse[m] = jnp.where(rid == t, recip, inverse[m])
                factor = jnp.where(rid > t, col[t] * recip, 0.0)
                for later in range(t + 1, BLOCK):
                    col[later] = col[later] - factor * col[later][t : t + 1, :]
                rows[m] = rows[m] - factor * rows[m][t : t + 1, :]
        for w, r, inv in zip(ws, rows, inverse):
            w[pl.ds(base, BLOCK), :] = r
            left = jnp.where(lane >= base + BLOCK, r[:, 0:n] * inv, 0.0)
            w[...] = w[...] - dot(left, r, 0, 0, HIGH)
        return carry

    lax.fori_loop(low, high, body, 0)


def identity(n):
    return (
        lax.broadcasted_iota(jnp.int32, (n, n), 0) == lax.broadcasted_iota(jnp.int32, (n, n), 1)
    ).astype(F32)


def load(w, a):
    n = w.shape[0]
    w[:, 0:n] = a
    w[:, n : 2 * n] = identity(n)


def factor_inverse(w):
    n = w.shape[0]
    diag = jnp.sum(w[:, 0:n] * identity(n), axis=1, keepdims=True)
    return w[:, n : 2 * n] * lax.rsqrt(diag)


def halves(a):
    high = a.astype(BF16)
    return high, (a - high.astype(F32)).astype(BF16)


def padded(rows, devices):
    unit = 8 * devices
    return -(-rows // unit) * unit


def comm_kernel(
    devices, n_cells, n_sched,
    cell_ref, core_matrix_ref, rate_ref, well_ref, sched_hbm, prof_ref,
    cells_ref, rows_ref, core_ref,
    sched, tile, mix, cell_t, rates_t, kt, k_ref, k_low, gram,
    x, r0, r1, r2, l_acc, y_acc, l_t, l_perp, hot_own,
    wu, wv, inv,
    c_acc, c_core, c_half, c_rs, c_fin,
    g_acc, g_core, g_half, g_rs, g_fin,
    l_part, l_core, l_half, l_rs, l_fin,
    y_part, y_core, y_all, y_fin,
    load_sem, x_s, x_r, y1_s, y1_r, z_s, z_r,
    c_s, c_r, c_bs, c_br, g_s, g_r, g_bs, g_br, l_s, l_r, l_bs, l_br,
    y_s, y_r, yb_s, yb_r,
):
    cells, n = cell_ref.shape
    block = rows_ref.shape[0]
    wells, profiles = rate_ref.shape
    depth = devices // 4
    chips = devices // 2
    sub = block // CHUNKS
    full = devices * sub
    me = lax.axis_index("cell")
    core = me % 2
    bit = (me // 2) % 2
    z = me // 4
    chip = me // 2
    mate = me + 1 - 2 * core
    across = me + 2 * (1 - 2 * bit)

    def on_chip(k):
        return ((chip + k) % chips) * 2 + core

    def on_line(k):
        return ((z + k) % depth) * 4 + me % 4

    barrier = pltpu.get_barrier_semaphore()
    for p in [mate] + [on_chip(k) for k in range(1, chips)]:
        pl.semaphore_signal(
            barrier, inc=1, device_id={"cell": p}, device_id_type=pl.DeviceIdType.MESH
        )

    loads = [
        pltpu.make_async_copy(
            sched_hbm.at[:, 2 * (g % 2) + g // 2],
            sched.at[pl.ds(g * depth, depth)],
            load_sem.at[g],
        )
        for g in range(4)
    ]
    for copy in loads:
        copy.start()

    def remote(src, dst, ssem, rsem, device):
        return pltpu.make_async_remote_copy(
            src_ref=src, dst_ref=dst, send_sem=ssem, recv_sem=rsem,
            device_id={"cell": device}, device_id_type=pl.DeviceIdType.MESH,
        )

    def part(i, size):
        return pl.ds(pl.multiple_of(i * size, size), size)


    def hop0(t):
        return remote(
            x.at[t, part(1 - core, full // 2)], r0.at[t], x_s.at[t], x_r.at[t], mate
        )

    def hop1(t):
        return remote(
            r0.at[t, part(1 - bit, full // 4)], r1.at[t], y1_s.at[t], y1_r.at[t], across
        )

    def hop2(t, k):
        return remote(
            r1.at[t, part((z + k) % depth, sub)], r2.at[t, k],
            z_s.at[t, k], z_r.at[t, k], on_line(k),
        )

    def fold0(t):
        hop0(t).wait_recv()
        r0[t] = (r0[t].astype(F32) + x[t, part(core, full // 2)].astype(F32)).astype(BF16)
        hop1(t).start()

    def fold1(t):
        hop1(t).wait_recv()
        r1[t] = (r1[t].astype(F32) + r0[t, part(bit, full // 4)].astype(F32)).astype(BF16)
        for k in range(1, depth):
            hop2(t, k).start()

    def fold2(t, acc, c):
        total = r1[t, part(z, sub)].astype(F32)
        for k in range(1, depth):
            hop2(t, k).wait_recv()
            total = total + r2[t, k].astype(F32)
        acc[part(c, sub)] = total


    small = {
        "c": (c_acc, c_core, c_half, c_rs, c_fin, c_s, c_r, c_bs, c_br),
        "g": (g_acc, g_core, g_half, g_rs, g_fin, g_s, g_r, g_bs, g_br),
        "l": (l_part, l_core, l_half, l_rs, l_fin, l_s, l_r, l_bs, l_br),
    }

    def step0(name):
        acc, got, _, _, _, ss, rs, _, _ = small[name]
        size = got.shape[0]
        return remote(acc.at[part(1 - core, size)], got, ss.at[0], rs.at[0], mate)

    def step1(name, k):
        _, _, half, slots, _, _, _, ss, rs = small[name]
        size = slots.shape[1]
        return remote(
            half.at[part((chip + k) % chips, size)], slots.at[k],
            ss.at[0, k], rs.at[0, k], on_chip(k),
        )

    def own_piece(name):
        _, _, _, slots, fin = small[name][:5]
        return fin.at[part(core * chips + chip, slots.shape[1])]

    def step2(name, k):
        ss, rs = small[name][7:]
        return remote(
            own_piece(name), own_piece(name), ss.at[1, k], rs.at[1, k], on_chip(k)
        )

    def step3(name):
        _, got, _, _, fin, ss, rs, _, _ = small[name]
        mine = fin.at[part(core, got.shape[0])]
        return remote(mine, mine, ss.at[1], rs.at[1], mate)

    def reduce_start(name, pieces):
        acc = small[name][0]
        base = 0
        for p in pieces:
            acc[base : base + p.shape[0]] = p
            base += p.shape[0]
        if base < acc.shape[0]:
            acc[base:] = jnp.zeros((acc.shape[0] - base, acc.shape[1]), F32)
        step0(name).start()

    def reduce_chips(name):
        acc, got, half = small[name][:3]
        step0(name).wait_recv()
        half[...] = acc[part(core, got.shape[0])] + got[...]
        for k in range(1, chips):
            step1(name, k).start()

    def reduce_share(name):
        _, _, half, slots, _ = small[name][:5]
        total = half[part(chip, slots.shape[1])]
        for k in range(1, chips):
            step1(name, k).wait_recv()
            total = total + slots[k]
        own_piece(name)[...] = total
        for k in range(1, chips):
            step2(name, k).start()

    def reduce_mate(name):
        for k in range(1, chips):
            step2(name, k).wait_recv()
        step3(name).start()

    def reduce_done(name):
        step3(name).wait_recv()

    def block_of(name, i):
        return small[name][4][i * n : (i + 1) * n]


    cell_f = cell_ref[...].astype(F32)
    mix[...] = (0.5 * dot(cell_f, core_matrix_ref[...], 1, 0, HIGH)).astype(BF16)
    cell_t[...] = cell_f.T.astype(BF16)
    hot_well = (
        lax.broadcasted_iota(jnp.int32, (wells, cells), 0) == well_ref[...]
    ).astype(F32).astype(BF16)
    rates_t[...] = (
        0.5 * TIME_STEP * dot(rate_ref[...].astype(F32).T.astype(BF16), hot_well, 1, 0)
    ).astype(BF16)
    kt[...] = jnp.zeros_like(kt)
    gram[...] = jnp.zeros_like(gram)
    hot_own[...] = (
        lax.broadcasted_iota(jnp.int32, (profiles, block), 0) == prof_ref[me]
    ).astype(F32).T.astype(BF16)
    for copy in loads:
        copy.wait()

    per = devices // CHUNKS

    def build(c):
        s = sched[:, part(c, sub), :].reshape(full, n)
        half = dot(s, mix[...], 1, 1)
        state = (half * ((1.0 + TIME_STEP) - (4.0 * TIME_STEP) * (half * half))).astype(BF16)
        tile[c] = state
        kt[...] += dot(s.astype(F32).T.astype(BF16), state, 1, 0)
        x[c] = dot(cell_t[...], state, 1, 1).T.astype(BF16)
        for g in range(per):
            p = c * per + g
            owner = (p % depth) * 4 + ((p // depth) % 2) * 2 + p // (2 * depth)
            rows = sched[p]
            hot = (
                lax.broadcasted_iota(jnp.int32, (profiles, block), 0) == prof_ref[owner]
            ).astype(F32).astype(BF16)
            both = jnp.concatenate([rows.astype(F32).T.astype(BF16), hot], axis=0)
            gram[...] += dot(both, rows, 1, 0)

    build(0)
    pl.semaphore_wait(barrier, chips)
    hop0(0).start()
    reduce_start(
        "c", [dot(cell_t[...], cell_ref[...], 1, 0), dot(rates_t[...], cell_ref[...], 1, 0)]
    )

    def phase(c, carry):
        build(c)
        hop0(c).start()
        fold0(c - 1)
        pl.when(c == 1)(lambda: reduce_chips("c"))
        pl.when(c == 4)(lambda: reduce_share("c"))
        pl.when(c == 7)(lambda: reduce_mate("c"))
        pl.when(c >= 3)(lambda: fold1(c - 3))
        pl.when(c >= 5)(lambda: fold2(c - 5, l_acc, c - 5))
        return carry

    lax.fori_loop(1, CHUNKS, phase, 0)

    high, low = halves(gram[n:].T)
    k_t = (kt[...] + dot(high, rates_t[...], 1, 0) + dot(low, rates_t[...], 1, 0)) * (
        2.0 * PANEL_SCALE / n_sched
    )
    k = k_t.T
    k_ref[...] = k
    k_low[...] = k.astype(BF16)
    both = jnp.concatenate([cell_t[...].astype(F32), k_t], axis=0)
    reduce_start("g", [dot(both, k_t, 1, 1, HIGH), dot(rates_t[...], k_low[...], 1, 0)])
    fold0(CHUNKS - 1)

    def project(c):
        x[CHUNKS + c] = dot(tile[c], k_low[...], 1, 0).astype(BF16)
        hop0(CHUNKS + c).start()

    def add_hot(acc, table):
        high, low = halves(table)
        both = dot(hot_own[...], jnp.concatenate([high, low], axis=1), 1, 0)
        return acc + both[:, 0:n] + both[:, n:]

    def y_fold1(c):
        fold1(CHUNKS + c)

    def y_fold2(c):
        fold2(CHUNKS + c, y_acc, c)

    def l_fold2(c):
        fold2(c, l_acc, c)

    project(0)
    fold1(CHUNKS - 3)
    l_fold2(CHUNKS - 5)
    project(1)
    fold0(CHUNKS)
    reduce_chips("g")
    reduce_done("c")
    project(2)
    fold0(CHUNKS + 1)
    fold1(CHUNKS - 2)
    l_fold2(CHUNKS - 4)
    project(3)
    fold0(CHUNKS + 2)
    project(4)
    fold0(CHUNKS + 3)
    l_fold2(CHUNKS - 3)
    fold1(CHUNKS - 1)
    project(5)
    fold0(CHUNKS + 4)
    project(6)
    fold0(CHUNKS + 5)
    l_fold2(CHUNKS - 2)
    reduce_share("g")
    project(7)
    fold0(CHUNKS + 6)
    fold0(CHUNKS + 7)
    y_fold1(0)
    l_fold2(CHUNKS - 1)

    left = add_hot(l_acc[...], block_of("c", 1)) * (2.0 * PANEL_SCALE / n_cells)
    l_t[...] = left.T
    reduce_start("l", [dot(l_t[...], l_t[...], 1, 1, HIGH)])

    pieces = n // BLOCK
    size_u = float(n_cells) ** 0.5
    size_v = float(n_sched) ** 0.5
    load(wu, block_of("c", 0))
    load(wv, gram[0:n])
    y_fold1(1)
    eliminate([wu, wv], 0, pieces // 4)
    reduce_chips("l")
    y_fold1(2)
    y_fold2(0)
    reduce_mate("g")
    eliminate([wu, wv], pieces // 4, pieces // 2)
    y_fold1(3)
    y_fold2(1)
    eliminate([wu, wv], pieces // 2, 3 * pieces // 4)
    reduce_done("g")
    y_fold1(4)
    y_fold2(2)
    eliminate([wu, wv], 3 * pieces // 4, pieces)
    reduce_share("l")
    y_fold1(5)
    y_fold2(3)
    inv[0] = factor_inverse(wu)
    inv[3] = factor_inverse(wv)
    ck = block_of("g", 0)
    kk = block_of("g", 1)

    def project_out(slot, side):
        a = dot(inv[slot], side, 1, 0, HIGH)
        inv[slot + 1] = dot(a, inv[slot], 0, 0, HIGH)
        return dot(a, a, 0, 0, HIGH)

    load(wu, kk - project_out(0, ck))
    group = bit + 2 * core
    own = sched[group * depth + z].astype(F32)
    overlap = project_out(3, ck.T * (n_sched / n_cells))
    l_perp[...] = l_t[...] - dot(inv[4], own, 1, 1, HIGH)
    y_fold1(6)
    y_fold2(4)
    eliminate([wu], 0, pieces // 2)
    y_fold1(7)
    y_fold2(5)
    reduce_mate("l")
    eliminate([wu], pieces // 2, pieces)
    y_fold2(6)
    inv[2] = factor_inverse(wu)
    inv[1] = -dot(inv[2], inv[1], 1, 0, HIGH)
    reduce_done("l")
    ll = l_fin[0:n]
    load(wv, ll - overlap)
    y_fold2(7)

    def y_step0():
        size = y_core.shape[0]
        return remote(y_part.at[part(1 - core, size)], y_core, y_s.at[0], y_r.at[0], mate)

    def y_step1(k):
        return remote(y_all.at[chip], y_all.at[chip], yb_s.at[k], yb_r.at[k], on_chip(k))

    def y_step2():
        mine = y_fin.at[part(core, y_core.shape[0])]
        return remote(mine, mine, y_s.at[1], y_r.at[1], mate)

    right = add_hot(y_acc[...], block_of("g", 2))
    moved = dot(inv[2], 2.0 * right, 1, 1, HIGH) + dot(
        inv[1], l_t[...] * (n_cells / PANEL_SCALE), 1, 0, HIGH
    )
    y_part[...] = dot(moved, l_perp[...], 1, 1, HIGH)
    y_step0().start()
    eliminate([wv], 0, pieces // 4)
    y_step0().wait_recv()
    y_all[chip] = (y_part[part(core, y_core.shape[0])] + y_core[...]).astype(BF16)
    for k in range(1, chips):
        y_step1(k).start()
    eliminate([wv], pieces // 4, pieces)
    inv[5] = factor_inverse(wv)
    inv[4] = -dot(inv[5], inv[4], 1, 0, HIGH)
    cells_ref[:, 0:n] = dot(cell_f, inv[0] * size_u, 1, 1, HIGH)
    cells_ref[:, n:] = dot(cell_f, inv[1] * size_u, 1, 1, HIGH) + dot(
        k_ref[...], inv[2] * size_u, 1, 1, HIGH
    )
    u11, u21, u22, v11, v21, v22 = [inv[i] for i in range(6)]
    rows_ref[:, 0:n] = dot(own, v11 * size_v, 1, 1, HIGH)
    rows_ref[:, n:] = dot(l_perp[...].T, v22 * size_v, 1, 1, HIGH)
    k_unscale = n_sched / PANEL_SCALE
    l_unscale = n_cells / PANEL_SCALE
    m11 = ck * k_unscale
    m12 = ll * l_unscale
    m21 = kk * k_unscale
    t11 = dot(u11, m11, 1, 0, HIGH)
    t12 = dot(u11, m12, 1, 0, HIGH)
    t21 = dot(u21, m11, 1, 0, HIGH) + dot(u22, m21, 1, 0, HIGH)
    scale = n / (float(n_cells) * float(n_sched)) ** 0.5
    core_ref[0:n, 0:n] = scale * dot(t11, v11, 1, 1, HIGH)
    core_ref[n:, 0:n] = scale * dot(t21, v11, 1, 1, HIGH)
    core_ref[0:n, n:] = scale * (dot(t11, v21, 1, 1, HIGH) + dot(t12, v22, 1, 1, HIGH))
    for k in range(1, chips):
        y_step1(k).wait_recv()
    total = y_all[0].astype(F32)
    for i in range(1, chips):
        total = total + y_all[i].astype(F32)
    y_fin[part(core, y_core.shape[0])] = total
    y_step2().start()
    y_step2().wait_recv()
    core_ref[n:, n:] = scale * dot(y_fin[...], v22, 1, 1, HIGH)

    def drain(t, carry):
        hop0(t).wait_send()
        hop1(t).wait_send()
        for k in range(1, depth):
            hop2(t, k).wait_send()
        return carry

    lax.fori_loop(0, 2 * CHUNKS, drain, 0)
    for name in small:
        step0(name).wait_send()
        for k in range(1, chips):
            step1(name, k).wait_send()
            step2(name, k).wait_send()
        step3(name).wait_send()
    y_step0().wait_send()
    for k in range(1, chips):
        y_step1(k).wait_send()
    y_step2().wait_send()


def hand_on(*refs):
    half = len(refs) // 2
    for source, target in zip(refs[:half], refs[half:]):
        target[...] = source[...]


def local(cell_factor, sched_factor, core_matrix, rate_table, cell_well, sched_profile):
    cells, n = cell_factor.shape
    n_sched = sched_factor.shape[0]
    devices = lax.axis_size("cell")
    n_cells = cells * devices
    block = n_sched // devices
    wells, profiles = rate_table.shape
    depth = devices // 4
    chips = devices // 2
    sub = block // CHUNKS
    full = devices * sub
    sds = jax.ShapeDtypeStruct
    vmem = pl.BlockSpec(memory_space=pltpu.VMEM)
    dma = pltpu.SemaphoreType.DMA
    both = 2 * CHUNKS

    def reduced(rows):
        size = padded(rows, devices)
        return [
            pltpu.VMEM((size, n), F32),
            pltpu.VMEM((size // 2, n), F32),
            pltpu.VMEM((size // 2, n), F32),
            pltpu.VMEM((chips, size // devices, n), F32),
            pltpu.VMEM((size, n), F32),
        ]

    outs = pl.pallas_call(
        functools.partial(comm_kernel, devices, n_cells, n_sched),
        in_specs=[vmem] * 4 + [pl.BlockSpec(memory_space=pltpu.HBM), vmem],
        out_specs=[vmem] * 3,
        out_shape=[
            pltpu.VMEM((cells, 2 * n), F32),
            pltpu.VMEM((block, 2 * n), F32),
            pltpu.VMEM((2 * n, 2 * n), F32),
        ],
        scratch_shapes=[
            pltpu.VMEM((devices, block, n), BF16),
            pltpu.VMEM((CHUNKS, full, cells), BF16),
            pltpu.VMEM((cells, n), BF16),
            pltpu.VMEM((n, cells), BF16),
            pltpu.VMEM((profiles, cells), BF16),
            pltpu.VMEM((n, cells), F32),
            pltpu.VMEM((cells, n), F32),
            pltpu.VMEM((cells, n), BF16),
            pltpu.VMEM((n + profiles, n), F32),
            pltpu.VMEM((both, full, n), BF16),
            pltpu.VMEM((both, full // 2, n), BF16),
            pltpu.VMEM((both, full // 4, n), BF16),
            pltpu.VMEM((both, depth, sub, n), BF16),
            pltpu.VMEM((block, n), F32),
            pltpu.VMEM((block, n), F32),
            pltpu.VMEM((n, block), F32),
            pltpu.VMEM((n, block), F32),
            pltpu.VMEM((block, profiles), BF16),
            pltpu.VMEM((n, 2 * n), F32),
            pltpu.VMEM((n, 2 * n), F32),
            pltpu.VMEM((6, n, n), F32),
        ]
        + reduced(n + profiles)
        + reduced(2 * n + profiles)
        + reduced(n)
        + [
            pltpu.VMEM((n, n), F32),
            pltpu.VMEM((n // 2, n), F32),
            pltpu.VMEM((chips, n // 2, n), BF16),
            pltpu.VMEM((n, n), F32),
            dma((4,)),
            dma((both,)), dma((both,)), dma((both,)), dma((both,)),
            dma((both, depth)), dma((both, depth)),
        ]
        + [dma((2,)), dma((2,)), dma((2, chips)), dma((2, chips))] * 3
        + [dma((2,)), dma((2,)), dma((chips,)), dma((chips,))],
        compiler_params=pltpu.CompilerParams(
            collective_id=0, has_side_effects=True, vmem_limit_bytes=VMEM_LIMIT
        ),
    )(
        *(
            pltpu.with_memory_space_constraint(a, pltpu.HBM)
            for a in (
                cell_factor, core_matrix, rate_table, cell_well.reshape(1, cells),
                sched_factor.reshape(depth, 4, block, n),
                sched_profile.reshape(devices, 1, block),
            )
        )
    )
    return tuple(
        pl.pallas_call(
            hand_on,
            in_specs=[vmem] * 3,
            out_specs=[vmem] * 3,
            out_shape=[sds(o.shape, o.dtype) for o in outs],
            compiler_params=pltpu.CompilerParams(vmem_limit_bytes=HAND_LIMIT),
        )(*outs)
    )


def solution(mesh):
    return jax.shard_map(
        local,
        mesh=mesh,
        in_specs=(
            P(("group", "cell"), None),
            P("group", None),
            P("group", None),
            P(),
            P(("group", "cell")),
            P("group"),
        ),
        out_specs=(P(("group", "cell"), None), P(("group", "cell"), None), P("group", None)),
        check_vma=False,
    )
```

```python
import functools

import jax
import jax.numpy as jnp
from jax import lax
from jax.experimental import pallas as pl
from jax.experimental.pallas import tpu as pltpu
from jax.sharding import PartitionSpec as P

TIME_STEP = 0.25
PANEL_SCALE = 8.0
HIGH = lax.Precision.HIGHEST
F32 = jnp.float32
BF16 = jnp.bfloat16
CHUNKS = 8
BLOCK = 16
WIDE = 32
AHEAD = 1
LAG1 = 4
LAG2 = 7
VMEM_LIMIT = 48 * 1000 * 1000
HAND_LIMIT = 16 * 1000 * 1000


def dot(a, b, ca, cb, precision=None):
    return lax.dot_general(
        a, b, (((ca,), (cb,)), ((), ())), precision=precision, preferred_element_type=F32
    )


def halves(a):
    high = a.astype(BF16)
    return high, (a - high.astype(F32)).astype(BF16)


def dot2(a, b, ca, cb):
    high, low = halves(b)
    return dot(a, high, ca, cb) + dot(a, low, ca, cb)


def dot3(a, b, ca, cb):
    high, low = halves(a)
    other, rest = halves(b)
    return dot(high, other, ca, cb) + (dot(high, rest, ca, cb) + dot(low, other, ca, cb))


def eliminate(ws, b, size, product):
    n = ws[0].shape[0]
    lane = lax.broadcasted_iota(jnp.int32, (1, n), 1)
    rid = lax.broadcasted_iota(jnp.int32, (size, 1), 0)
    base = b * size
    top = base + size
    rows = [w[base:top, :] for w in ws]
    cols = [
        [
            jnp.sum(jnp.where(lane == base + t, r[:, 0:n], 0.0), axis=1, keepdims=True)
            for t in range(size)
        ]
        for r in rows
    ]
    inverse = [jnp.zeros((size, 1), F32) for _ in ws]
    for t in range(size):
        for m in range(len(ws)):
            col = cols[m]
            recip = 1.0 / col[t][t : t + 1, :]
            inverse[m] = jnp.where(rid == t, recip, inverse[m])
            factor = jnp.where(rid > t, col[t] * recip, 0.0)
            for later in range(t + 1, size):
                col[later] = col[later] - factor * col[later][t : t + 1, :]
            rows[m] = rows[m] - factor * rows[m][t : t + 1, :]
    for w, r, inv in zip(ws, rows, inverse):
        w[base:top, :] = r
        if top < n:
            w[top:, :] = w[top:, :] - product(r[:, 0:n] * inv, r, 0, 0)[top:, :]


def exact(a, b, ca, cb):
    return dot(a, b, ca, cb, HIGH)


def identity(n):
    return (
        lax.broadcasted_iota(jnp.int32, (n, n), 0) == lax.broadcasted_iota(jnp.int32, (n, n), 1)
    ).astype(F32)


def load(w, a):
    n = w.shape[0]
    w[:, 0:n] = a
    w[:, n : 2 * n] = identity(n)


def factor_inverse(w):
    n = w.shape[0]
    diag = jnp.sum(w[:, 0:n] * identity(n), axis=1, keepdims=True)
    return w[:, n : 2 * n] * lax.rsqrt(diag)


def padded(rows, devices):
    unit = 8 * devices
    return -(-rows // unit) * unit


def comm_kernel(
    devices, n_cells, n_sched,
    cell_hbm, core_matrix_hbm, rate_hbm, well_hbm, sched_hbm, prof_hbm,
    cells_ref, rows_ref, core_ref,
    cell_ref, core_matrix_ref, rate_ref, well_ref, prof_ref, sched, tile, mix, cell_t, rates_t, kt, k_ref, k_low, gram,
    x, r0, r1, r2, l_acc, y_acc, l_t, l_perp, hot_own,
    wu, wv, inv,
    c_acc, c_core, c_half, c_rs, c_fin,
    g_acc, g_core, g_half, g_rs, g_fin,
    l_part, l_core, l_half, l_rs, l_fin,
    y_part, y_core, y_all, y_fin,
    load_sem, x_s, x_r, y1_s, y1_r, z_s, z_r,
    c_s, c_r, c_bs, c_br, g_s, g_r, g_bs, g_br, l_s, l_r, l_bs, l_br,
    y_s, y_r, yb_s, yb_r,
):
    cells, n = cell_ref.shape
    block = rows_ref.shape[0]
    wells, profiles = rate_ref.shape
    depth = devices // 4
    chips = devices // 2
    sub = block // CHUNKS
    full = devices * sub
    me = lax.axis_index("cell")
    core = me % 2
    bit = (me // 2) % 2
    z = me // 4
    chip = me // 2
    mate = me + 1 - 2 * core
    across = me + 2 * (1 - 2 * bit)

    def on_chip(k):
        return ((chip + k) % chips) * 2 + core

    def on_line(k):
        return ((z + k) % depth) * 4 + me % 4

    barrier = pltpu.get_barrier_semaphore()
    for p in [mate] + [on_chip(k) for k in range(1, chips)]:
        pl.semaphore_signal(
            barrier, inc=1, device_id={"cell": p}, device_id_type=pl.DeviceIdType.MESH
        )

    early = [
        pltpu.make_async_copy(source, target, load_sem.at[4 + i])
        for i, (source, target) in enumerate(
            [
                (cell_hbm, cell_ref), (core_matrix_hbm, core_matrix_ref), (rate_hbm, rate_ref),
                (well_hbm, well_ref), (prof_hbm, prof_ref),
            ]
        )
    ]
    for copy in early:
        copy.start()
    loads = [
        pltpu.make_async_copy(
            sched_hbm.at[:, 2 * (g % 2) + g // 2],
            sched.at[pl.ds(g * depth, depth)],
            load_sem.at[g],
        )
        for g in range(4)
    ]
    for copy in loads:
        copy.start()

    def remote(src, dst, ssem, rsem, device):
        return pltpu.make_async_remote_copy(
            src_ref=src, dst_ref=dst, send_sem=ssem, recv_sem=rsem,
            device_id={"cell": device}, device_id_type=pl.DeviceIdType.MESH,
        )

    def part(i, size):
        return pl.ds(pl.multiple_of(i * size, size), size)


    def hop0(t):
        return remote(
            x.at[t, part(1 - core, full // 2)], r0.at[t], x_s.at[t], x_r.at[t], mate
        )

    def hop1(t):
        return remote(
            r0.at[t, part(1 - bit, full // 4)], r1.at[t], y1_s.at[t], y1_r.at[t], across
        )

    def hop2(t, k):
        return remote(
            r1.at[t, part((z + k) % depth, sub)], r2.at[t, k],
            z_s.at[t, k], z_r.at[t, k], on_line(k),
        )

    def fold0(t):
        hop0(t).wait_recv()
        r0[t] = (r0[t].astype(F32) + x[t, part(core, full // 2)].astype(F32)).astype(BF16)
        hop1(t).start()

    def fold1(t):
        hop1(t).wait_recv()
        r1[t] = (r1[t].astype(F32) + r0[t, part(bit, full // 4)].astype(F32)).astype(BF16)
        for k in range(1, depth):
            hop2(t, k).start()

    def fold2(t, acc, c):
        total = r1[t, part(z, sub)].astype(F32)
        for k in range(1, depth):
            hop2(t, k).wait_recv()
            total = total + r2[t, k].astype(F32)
        acc[part(c, sub)] = total


    small = {
        "c": (c_acc, c_core, c_half, c_rs, c_fin, c_s, c_r, c_bs, c_br),
        "g": (g_acc, g_core, g_half, g_rs, g_fin, g_s, g_r, g_bs, g_br),
        "l": (l_part, l_core, l_half, l_rs, l_fin, l_s, l_r, l_bs, l_br),
    }

    def step0(name):
        acc, got, _, _, _, ss, rs, _, _ = small[name]
        size = got.shape[0]
        return remote(acc.at[part(1 - core, size)], got, ss.at[0], rs.at[0], mate)

    def step1(name, k):
        _, _, half, slots, _, _, _, ss, rs = small[name]
        size = slots.shape[1]
        return remote(
            half.at[part((chip + k) % chips, size)], slots.at[k],
            ss.at[0, k], rs.at[0, k], on_chip(k),
        )

    def own_piece(name):
        _, _, _, slots, fin = small[name][:5]
        return fin.at[part(core * chips + chip, slots.shape[1])]

    def step2(name, k):
        ss, rs = small[name][7:]
        return remote(
            own_piece(name), own_piece(name), ss.at[1, k], rs.at[1, k], on_chip(k)
        )

    def step3(name):
        _, got, _, _, fin, ss, rs, _, _ = small[name]
        mine = fin.at[part(core, got.shape[0])]
        return remote(mine, mine, ss.at[1], rs.at[1], mate)

    def reduce_start(name, pieces):
        acc = small[name][0]
        base = 0
        for p in pieces:
            acc[base : base + p.shape[0]] = p
            base += p.shape[0]
        if base < acc.shape[0]:
            acc[base:] = jnp.zeros((acc.shape[0] - base, acc.shape[1]), F32)
        step0(name).start()

    def reduce_chips(name):
        acc, got, half = small[name][:3]
        step0(name).wait_recv()
        half[...] = acc[part(core, got.shape[0])] + got[...]
        for k in range(1, chips):
            step1(name, k).start()

    def reduce_share(name):
        _, _, half, slots, _ = small[name][:5]
        total = half[part(chip, slots.shape[1])]
        for k in range(1, chips):
            step1(name, k).wait_recv()
            total = total + slots[k]
        own_piece(name)[...] = total
        for k in range(1, chips):
            step2(name, k).start()

    def reduce_mate(name):
        for k in range(1, chips):
            step2(name, k).wait_recv()
        step3(name).start()

    def reduce_done(name):
        step3(name).wait_recv()

    def block_of(name, i):
        return small[name][4][i * n : (i + 1) * n]


    for copy in early:
        copy.wait()
    cell_f = cell_ref[...].astype(F32)
    mix[...] = (0.5 * dot(cell_f, core_matrix_ref[...], 1, 0, HIGH)).astype(BF16)
    cell_t[...] = cell_f.T.astype(BF16)
    hot_well = (
        lax.broadcasted_iota(jnp.int32, (wells, cells), 0) == well_ref[...]
    ).astype(F32).astype(BF16)
    rates_t[...] = (
        0.5 * TIME_STEP * dot(rate_ref[...].astype(F32).T.astype(BF16), hot_well, 1, 0)
    ).astype(BF16)
    kt[...] = jnp.zeros_like(kt)
    gram[...] = jnp.zeros_like(gram)
    hot_own[...] = (
        lax.broadcasted_iota(jnp.int32, (profiles, block), 0) == prof_ref[me]
    ).astype(F32).T.astype(BF16)
    for copy in loads:
        copy.wait()

    per = devices // CHUNKS

    def build(c):
        s = sched[:, part(c, sub), :].reshape(full, n)
        half = dot(s, mix[...], 1, 1)
        state = (half * ((1.0 + TIME_STEP) - (4.0 * TIME_STEP) * (half * half))).astype(BF16)
        tile[c] = state
        kt[...] += dot(s.astype(F32).T.astype(BF16), state, 1, 0)
        x[c] = dot(cell_t[...], state, 1, 1).T.astype(BF16)
        for g in range(per):
            p = c * per + g
            owner = (p % depth) * 4 + ((p // depth) % 2) * 2 + p // (2 * depth)
            rows = sched[p]
            hot = (
                lax.broadcasted_iota(jnp.int32, (profiles, block), 0) == prof_ref[owner]
            ).astype(F32).astype(BF16)
            both = jnp.concatenate([rows.astype(F32).T.astype(BF16), hot], axis=0)
            gram[...] += dot(both, rows, 1, 0)

    def ahead(c, carry):
        build(c)
        return carry

    lax.fori_loop(0, AHEAD, ahead, 0)
    pl.semaphore_wait(barrier, chips)
    for c in range(AHEAD):
        hop0(c).start()
    reduce_start(
        "c", [dot(cell_t[...], cell_ref[...], 1, 0), dot(rates_t[...], cell_ref[...], 1, 0)]
    )
    for c in range(AHEAD - 1):
        fold0(c)

    def phase(c, carry):
        build(c)
        hop0(c).start()
        fold0(c - 1)
        pl.when(c == AHEAD)(lambda: reduce_chips("c"))
        pl.when(c == AHEAD + 2)(lambda: reduce_share("c"))
        pl.when(c == AHEAD + 4)(lambda: reduce_mate("c"))
        pl.when(c >= LAG1)(lambda: fold1(c - LAG1))
        pl.when(c >= LAG2)(lambda: fold2(c - LAG2, l_acc, c - LAG2))
        return carry

    lax.fori_loop(AHEAD, CHUNKS, phase, 0)

    fold1(CHUNKS - 4)
    fold2(1, l_acc, 1)
    high, low = halves(gram[n:].T)
    k_t = (kt[...] + dot(high, rates_t[...], 1, 0) + dot(low, rates_t[...], 1, 0)) * (
        2.0 * PANEL_SCALE / n_sched
    )
    k = k_t.T
    k_ref[...] = k
    k_low[...] = k.astype(BF16)
    fold0(CHUNKS - 1)
    both = jnp.concatenate([cell_t[...].astype(F32), k_t], axis=0)
    reduce_start("g", [dot3(both, k_t, 1, 1), dot(rates_t[...], k_low[...], 1, 0)])

    def project(c, *blocks):
        y = dot(tile[c], k_low[...], 1, 0)
        for b in blocks:
            eliminate([wu, wv], b, BLOCK, exact)
        x[CHUNKS + c] = y.astype(BF16)
        hop0(CHUNKS + c).start()

    def add_hot(acc, table):
        high, low = halves(table)
        both = dot(hot_own[...], jnp.concatenate([high, low], axis=1), 1, 0)
        return acc + both[:, 0:n] + both[:, n:]

    def y_fold1(c):
        fold1(CHUNKS + c)

    def y_fold2(c):
        fold2(CHUNKS + c, y_acc, c)

    def l_fold2(c):
        fold2(c, l_acc, c)

    reduce_done("c")
    load(wu, block_of("c", 0))
    load(wv, gram[0:n])
    pieces = n // BLOCK
    wide = n // WIDE
    ahead_of = [range(pieces * c // CHUNKS, pieces * (c + 1) // CHUNKS) for c in range(CHUNKS)]
    project(0, *ahead_of[0])
    fold1(CHUNKS - 3)
    l_fold2(2)
    project(1, *ahead_of[1])
    fold0(CHUNKS)
    reduce_chips("g")
    project(2, *ahead_of[2])
    fold0(CHUNKS + 1)
    fold1(CHUNKS - 2)
    l_fold2(3)
    project(3, *ahead_of[3])
    fold0(CHUNKS + 2)
    project(4, *ahead_of[4])
    fold0(CHUNKS + 3)
    fold1(CHUNKS - 1)
    l_fold2(4)
    project(5, *ahead_of[5])
    fold0(CHUNKS + 4)
    project(6, *ahead_of[6])
    fold0(CHUNKS + 5)
    l_fold2(5)
    y_fold1(0)
    project(7, *ahead_of[7])
    fold0(CHUNKS + 6)
    reduce_share("g")
    l_fold2(6)
    y_fold1(1)
    fold0(CHUNKS + 7)
    l_fold2(7)

    left = add_hot(l_acc[...], block_of("c", 1)) * (2.0 * PANEL_SCALE / n_cells)
    l_t[...] = left.T
    reduce_start("l", [dot3(l_t[...], l_t[...], 1, 1)])

    size_u = float(n_cells) ** 0.5
    size_v = float(n_sched) ** 0.5
    inv[0] = factor_inverse(wu)
    inv[3] = factor_inverse(wv)
    own = sched[(bit + 2 * core) * depth + z]
    y_fold1(2)
    reduce_mate("g")
    reduce_chips("l")
    rows_ref[:, 0:n] = dot2(own, inv[3] * size_v, 1, 1)
    y_fold1(3)
    y_fold2(0)
    reduce_done("g")
    ck = block_of("g", 0)
    kk = block_of("g", 1)

    def project_out(slot, side):
        a = dot3(inv[slot], side, 1, 0)
        inv[slot + 1] = dot3(a, inv[slot], 0, 0)
        return dot3(a, a, 0, 0)

    load(wu, kk - project_out(0, ck))
    overlap = project_out(3, ck.T * (n_sched / n_cells))
    l_perp[...] = l_t[...] - dot(inv[4], own.astype(F32), 1, 1, HIGH)
    y_fold1(4)
    y_fold2(1)
    for b in range(wide // 2):
        eliminate([wu], b, WIDE, dot3)
    reduce_share("l")
    y_fold1(5)
    y_fold2(2)
    for b in range(wide // 2, wide):
        eliminate([wu], b, WIDE, dot3)
    inv[2] = factor_inverse(wu)
    inv[1] = -dot(inv[2], inv[1], 1, 0, HIGH)
    y_fold1(6)
    y_fold2(3)
    y_fold2(4)
    y_fold1(7)
    reduce_mate("l")
    def y_step0():
        size = y_core.shape[0]
        return remote(y_part.at[part(1 - core, size)], y_core, y_s.at[0], y_r.at[0], mate)

    def y_step1(k):
        return remote(y_all.at[chip], y_all.at[chip], yb_s.at[k], yb_r.at[k], on_chip(k))

    def y_step2():
        mine = y_fin.at[part(core, y_core.shape[0])]
        return remote(mine, mine, y_s.at[1], y_r.at[1], mate)

    reduce_done("l")
    ll = l_fin[0:n]
    load(wv, ll - overlap)
    eliminate([wv], 0, WIDE, dot3)
    y_fold2(5)
    y_fold2(6)
    y_fold2(7)

    right = add_hot(y_acc[...], block_of("g", 2))
    moved = dot3(inv[2], 2.0 * right, 1, 1) + dot3(
        inv[1], l_t[...] * (n_cells / PANEL_SCALE), 1, 0
    )
    y_part[...] = dot3(moved, l_perp[...], 1, 1)
    y_step0().start()
    for b in range(1, wide):
        eliminate([wv], b, WIDE, dot3)
    y_step0().wait_recv()
    y_all[chip] = (y_part[part(core, y_core.shape[0])] + y_core[...]).astype(BF16)
    for k in range(1, chips):
        y_step1(k).start()
    u11, u21, u22, v11 = [inv[i] for i in range(4)]
    v22 = factor_inverse(wv)
    v21 = -dot(v22, inv[4], 1, 0, HIGH)
    rows_ref[:, n:] = dot3(l_perp[...].T, v22 * size_v, 1, 1)
    k_unscale = n_sched / PANEL_SCALE
    l_unscale = n_cells / PANEL_SCALE
    scale = n / (float(n_cells) * float(n_sched)) ** 0.5
    t11 = dot3(u11, ck * k_unscale, 1, 0)
    t12 = dot3(u11, ll * l_unscale, 1, 0)
    t21 = dot3(u21, ck * k_unscale, 1, 0) + dot3(u22, kk * k_unscale, 1, 0)
    core_ref[0:n, 0:n] = scale * dot3(t11, v11, 1, 1)
    core_ref[n:, 0:n] = scale * dot3(t21, v11, 1, 1)
    core_ref[0:n, n:] = scale * (dot(t11, v21, 1, 1, HIGH) + dot(t12, v22, 1, 1, HIGH))
    cells_ref[:, 0:n] = dot2(cell_ref[...], u11 * size_u, 1, 1)
    cells_ref[:, n:] = dot2(cell_ref[...], u21 * size_u, 1, 1) + dot3(
        k_ref[...], u22 * size_u, 1, 1
    )
    def drain(t, carry):
        hop0(t).wait_send()
        hop1(t).wait_send()
        for k in range(1, depth):
            hop2(t, k).wait_send()
        return carry

    lax.fori_loop(0, 2 * CHUNKS, drain, 0)
    for name in small:
        step0(name).wait_send()
        for k in range(1, chips):
            step1(name, k).wait_send()
            step2(name, k).wait_send()
        step3(name).wait_send()
    for k in range(1, chips):
        y_step1(k).wait_recv()
    total = y_all[0].astype(F32)
    for i in range(1, chips):
        total = total + y_all[i].astype(F32)
    y_fin[part(core, y_core.shape[0])] = total
    y_step2().start()
    y_step2().wait_recv()
    core_ref[n:, n:] = scale * dot(y_fin[...], v22, 1, 1, HIGH)

    y_step0().wait_send()
    for k in range(1, chips):
        y_step1(k).wait_send()
    y_step2().wait_send()


def hand_on(*refs):
    half = len(refs) // 2
    for source, target in zip(refs[:half], refs[half:]):
        target[...] = source[...]


def local(cell_factor, sched_factor, core_matrix, rate_table, cell_well, sched_profile):
    cells, n = cell_factor.shape
    n_sched = sched_factor.shape[0]
    devices = lax.axis_size("cell")
    n_cells = cells * devices
    block = n_sched // devices
    wells, profiles = rate_table.shape
    depth = devices // 4
    chips = devices // 2
    sub = block // CHUNKS
    full = devices * sub
    sds = jax.ShapeDtypeStruct
    vmem = pl.BlockSpec(memory_space=pltpu.VMEM)
    dma = pltpu.SemaphoreType.DMA
    both = 2 * CHUNKS

    def reduced(rows):
        size = padded(rows, devices)
        return [
            pltpu.VMEM((size, n), F32),
            pltpu.VMEM((size // 2, n), F32),
            pltpu.VMEM((size // 2, n), F32),
            pltpu.VMEM((chips, size // devices, n), F32),
            pltpu.VMEM((size, n), F32),
        ]

    outs = pl.pallas_call(
        functools.partial(comm_kernel, devices, n_cells, n_sched),
        in_specs=[pl.BlockSpec(memory_space=pltpu.HBM)] * 6,
        out_specs=[vmem] * 3,
        out_shape=[
            pltpu.VMEM((cells, 2 * n), F32),
            pltpu.VMEM((block, 2 * n), F32),
            pltpu.VMEM((2 * n, 2 * n), F32),
        ],
        scratch_shapes=[
            pltpu.VMEM((cells, n), BF16),
            pltpu.VMEM((n, n), F32),
            pltpu.VMEM((wells, profiles), BF16),
            pltpu.VMEM((1, cells), jnp.int32),
            pltpu.VMEM((devices, 1, block), jnp.int32),
            pltpu.VMEM((devices, block, n), BF16),
            pltpu.VMEM((CHUNKS, full, cells), BF16),
            pltpu.VMEM((cells, n), BF16),
            pltpu.VMEM((n, cells), BF16),
            pltpu.VMEM((profiles, cells), BF16),
            pltpu.VMEM((n, cells), F32),
            pltpu.VMEM((cells, n), F32),
            pltpu.VMEM((cells, n), BF16),
            pltpu.VMEM((n + profiles, n), F32),
            pltpu.VMEM((both, full, n), BF16),
            pltpu.VMEM((both, full // 2, n), BF16),
            pltpu.VMEM((both, full // 4, n), BF16),
            pltpu.VMEM((both, depth, sub, n), BF16),
            pltpu.VMEM((block, n), F32),
            pltpu.VMEM((block, n), F32),
            pltpu.VMEM((n, block), F32),
            pltpu.VMEM((n, block), F32),
            pltpu.VMEM((block, profiles), BF16),
            pltpu.VMEM((n, 2 * n), F32),
            pltpu.VMEM((n, 2 * n), F32),
            pltpu.VMEM((6, n, n), F32),
        ]
        + reduced(n + profiles)
        + reduced(2 * n + profiles)
        + reduced(n)
        + [
            pltpu.VMEM((n, n), F32),
            pltpu.VMEM((n // 2, n), F32),
            pltpu.VMEM((chips, n // 2, n), BF16),
            pltpu.VMEM((n, n), F32),
            dma((9,)),
            dma((both,)), dma((both,)), dma((both,)), dma((both,)),
            dma((both, depth)), dma((both, depth)),
        ]
        + [dma((2,)), dma((2,)), dma((2, chips)), dma((2, chips))] * 3
        + [dma((2,)), dma((2,)), dma((chips,)), dma((chips,))],
        compiler_params=pltpu.CompilerParams(
            collective_id=0, has_side_effects=True, vmem_limit_bytes=VMEM_LIMIT
        ),
    )(
        *(
            pltpu.with_memory_space_constraint(a, pltpu.HBM)
            for a in (
                cell_factor, core_matrix, rate_table, cell_well.reshape(1, cells),
                sched_factor.reshape(depth, 4, block, n),
                sched_profile.reshape(devices, 1, block),
            )
        )
    )
    return tuple(
        pl.pallas_call(
            hand_on,
            in_specs=[vmem] * 3,
            out_specs=[vmem] * 3,
            out_shape=[sds(o.shape, o.dtype) for o in outs],
            compiler_params=pltpu.CompilerParams(vmem_limit_bytes=HAND_LIMIT),
        )(*outs)
    )


def solution(mesh):
    return jax.shard_map(
        local,
        mesh=mesh,
        in_specs=(
            P(("group", "cell"), None),
            P("group", None),
            P("group", None),
            P(),
            P(("group", "cell")),
            P("group"),
        ),
        out_specs=(P(("group", "cell"), None), P(("group", "cell"), None), P("group", None)),
        check_vma=False,
    )
```

```python
import functools

import jax
import jax.numpy as jnp
from jax import lax
from jax.experimental import pallas as pl
from jax.experimental.pallas import tpu as pltpu
from jax.sharding import PartitionSpec as P

TIME_STEP = 0.25
PANEL_SCALE = 8.0
HIGH = lax.Precision.HIGHEST
F32 = jnp.float32
BF16 = jnp.bfloat16
CHUNKS = 8
BLOCK = 16
WIDE = 32
AHEAD = 1
LAG1 = 3
LAG2 = 6
VMEM_LIMIT = 48 * 1000 * 1000
HAND_LIMIT = 16 * 1000 * 1000


def dot(a, b, ca, cb, precision=None):
    return lax.dot_general(
        a, b, (((ca,), (cb,)), ((), ())), precision=precision, preferred_element_type=F32
    )


def halves(a):
    high = a.astype(BF16)
    return high, (a - high.astype(F32)).astype(BF16)


def dot2(a, b, ca, cb):
    high, low = halves(b)
    return dot(a, high, ca, cb) + dot(a, low, ca, cb)


def dot3(a, b, ca, cb):
    high, low = halves(a)
    other, rest = halves(b)
    return dot(high, other, ca, cb) + (dot(high, rest, ca, cb) + dot(low, other, ca, cb))


def eliminate(ws, b, size, product):
    n = ws[0].shape[0]
    lane = lax.broadcasted_iota(jnp.int32, (1, n), 1)
    rid = lax.broadcasted_iota(jnp.int32, (size, 1), 0)
    base = b * size
    top = base + size
    rows = [w[base:top, :] for w in ws]
    cols = [
        [
            jnp.sum(jnp.where(lane == base + t, r[:, 0:n], 0.0), axis=1, keepdims=True)
            for t in range(size)
        ]
        for r in rows
    ]
    inverse = [jnp.zeros((size, 1), F32) for _ in ws]
    for t in range(size):
        for m in range(len(ws)):
            col = cols[m]
            recip = 1.0 / col[t][t : t + 1, :]
            inverse[m] = jnp.where(rid == t, recip, inverse[m])
            factor = jnp.where(rid > t, col[t] * recip, 0.0)
            for later in range(t + 1, size):
                col[later] = col[later] - factor * col[later][t : t + 1, :]
            rows[m] = rows[m] - factor * rows[m][t : t + 1, :]
    for w, r, inv in zip(ws, rows, inverse):
        w[base:top, :] = r
        if top < n:
            w[top:, :] = w[top:, :] - product(r[:, 0:n] * inv, r, 0, 0)[top:, :]


def exact(a, b, ca, cb):
    return dot(a, b, ca, cb, HIGH)


def identity(n):
    return (
        lax.broadcasted_iota(jnp.int32, (n, n), 0) == lax.broadcasted_iota(jnp.int32, (n, n), 1)
    ).astype(F32)


def load(w, a):
    n = w.shape[0]
    w[:, 0:n] = a
    w[:, n : 2 * n] = identity(n)


def factor_inverse(w):
    n = w.shape[0]
    diag = jnp.sum(w[:, 0:n] * identity(n), axis=1, keepdims=True)
    return w[:, n : 2 * n] * lax.rsqrt(diag)


def padded(rows, devices):
    unit = 8 * devices
    return -(-rows // unit) * unit


def comm_kernel(
    devices, n_cells, n_sched,
    cell_hbm, core_matrix_hbm, rate_hbm, well_hbm, sched_hbm, prof_hbm,
    cells_ref, rows_ref, core_ref,
    cell_ref, core_matrix_ref, rate_ref, well_ref, prof_ref, sched, tile, mix, cell_t, rates_t, kt, k_ref, k_low, gram,
    x, r0, r1, r2, l_acc, y_acc, l_t, l_perp, hot_own,
    wu, wv, inv,
    c_acc, c_core, c_half, c_rs, c_fin,
    g_acc, g_core, g_half, g_rs, g_fin,
    l_part, l_core, l_half, l_rs, l_fin,
    y_part, y_core, y_all, y_fin,
    load_sem, x_s, x_r, y1_s, y1_r, z_s, z_r,
    c_s, c_r, c_bs, c_br, g_s, g_r, g_bs, g_br, l_s, l_r, l_bs, l_br,
    y_s, y_r, yb_s, yb_r,
):
    cells, n = cell_ref.shape
    block = rows_ref.shape[0]
    wells, profiles = rate_ref.shape
    depth = devices // 4
    chips = devices // 2
    sub = block // CHUNKS
    full = devices * sub
    me = lax.axis_index("cell")
    core = me % 2
    bit = (me // 2) % 2
    z = me // 4
    chip = me // 2
    mate = me + 1 - 2 * core
    across = me + 2 * (1 - 2 * bit)

    def on_chip(k):
        return ((chip + k) % chips) * 2 + core

    def on_line(k):
        return ((z + k) % depth) * 4 + me % 4

    barrier = pltpu.get_barrier_semaphore()
    for p in [mate] + [on_chip(k) for k in range(1, chips)]:
        pl.semaphore_signal(
            barrier, inc=1, device_id={"cell": p}, device_id_type=pl.DeviceIdType.MESH
        )

    early = [
        pltpu.make_async_copy(source, target, load_sem.at[4 + i])
        for i, (source, target) in enumerate(
            [
                (cell_hbm, cell_ref), (core_matrix_hbm, core_matrix_ref), (rate_hbm, rate_ref),
                (well_hbm, well_ref), (prof_hbm, prof_ref),
            ]
        )
    ]
    for copy in early:
        copy.start()
    loads = [
        pltpu.make_async_copy(
            sched_hbm.at[:, 2 * (g % 2) + g // 2],
            sched.at[pl.ds(g * depth, depth)],
            load_sem.at[g],
        )
        for g in range(4)
    ]
    for copy in loads:
        copy.start()

    def remote(src, dst, ssem, rsem, device):
        return pltpu.make_async_remote_copy(
            src_ref=src, dst_ref=dst, send_sem=ssem, recv_sem=rsem,
            device_id={"cell": device}, device_id_type=pl.DeviceIdType.MESH,
        )

    def part(i, size):
        return pl.ds(pl.multiple_of(i * size, size), size)


    def hop0(t):
        return remote(
            x.at[t, part(1 - core, full // 2)], r0.at[t], x_s.at[t], x_r.at[t], mate
        )

    def hop1(t):
        return remote(
            r0.at[t, part(1 - bit, full // 4)], r1.at[t], y1_s.at[t], y1_r.at[t], across
        )

    def hop2(t, k):
        return remote(
            r1.at[t, part((z + k) % depth, sub)], r2.at[t, k],
            z_s.at[t, k], z_r.at[t, k], on_line(k),
        )

    def fold0(t):
        hop0(t).wait_recv()
        r0[t] = (r0[t].astype(F32) + x[t, part(core, full // 2)].astype(F32)).astype(BF16)
        hop1(t).start()

    def fold1(t):
        hop1(t).wait_recv()
        r1[t] = (r1[t].astype(F32) + r0[t, part(bit, full // 4)].astype(F32)).astype(BF16)
        for k in range(1, depth):
            hop2(t, k).start()

    def fold2(t, acc, c):
        total = r1[t, part(z, sub)].astype(F32)
        for k in range(1, depth):
            hop2(t, k).wait_recv()
            total = total + r2[t, k].astype(F32)
        acc[part(c, sub)] = total


    small = {
        "c": (c_acc, c_core, c_half, c_rs, c_fin, c_s, c_r, c_bs, c_br),
        "g": (g_acc, g_core, g_half, g_rs, g_fin, g_s, g_r, g_bs, g_br),
        "l": (l_part, l_core, l_half, l_rs, l_fin, l_s, l_r, l_bs, l_br),
    }

    def step0(name):
        acc, got, _, _, _, ss, rs, _, _ = small[name]
        size = got.shape[0]
        return remote(acc.at[part(1 - core, size)], got, ss.at[0], rs.at[0], mate)

    def step1(name, k):
        _, _, half, slots, _, _, _, ss, rs = small[name]
        size = slots.shape[1]
        return remote(
            half.at[part((chip + k) % chips, size)], slots.at[k],
            ss.at[0, k], rs.at[0, k], on_chip(k),
        )

    def own_piece(name):
        _, _, _, slots, fin = small[name][:5]
        return fin.at[part(core * chips + chip, slots.shape[1])]

    def step2(name, k):
        ss, rs = small[name][7:]
        return remote(
            own_piece(name), own_piece(name), ss.at[1, k], rs.at[1, k], on_chip(k)
        )

    def step3(name):
        _, got, _, _, fin, ss, rs, _, _ = small[name]
        mine = fin.at[part(core, got.shape[0])]
        return remote(mine, mine, ss.at[1], rs.at[1], mate)

    def reduce_start(name, pieces):
        acc = small[name][0]
        base = 0
        for p in pieces:
            acc[base : base + p.shape[0]] = p
            base += p.shape[0]
        if base < acc.shape[0]:
            acc[base:] = jnp.zeros((acc.shape[0] - base, acc.shape[1]), F32)
        step0(name).start()

    def reduce_chips(name):
        acc, got, half = small[name][:3]
        step0(name).wait_recv()
        half[...] = acc[part(core, got.shape[0])] + got[...]
        for k in range(1, chips):
            step1(name, k).start()

    def reduce_share(name):
        _, _, half, slots, _ = small[name][:5]
        total = half[part(chip, slots.shape[1])]
        for k in range(1, chips):
            step1(name, k).wait_recv()
            total = total + slots[k]
        own_piece(name)[...] = total
        for k in range(1, chips):
            step2(name, k).start()

    def reduce_mate(name):
        for k in range(1, chips):
            step2(name, k).wait_recv()
        step3(name).start()

    def reduce_done(name):
        step3(name).wait_recv()

    def block_of(name, i):
        return small[name][4][i * n : (i + 1) * n]


    for copy in early:
        copy.wait()
    cell_f = cell_ref[...].astype(F32)
    mix[...] = (0.5 * dot(cell_f, core_matrix_ref[...], 1, 0, HIGH)).astype(BF16)
    cell_t[...] = cell_f.T.astype(BF16)
    hot_well = (
        lax.broadcasted_iota(jnp.int32, (wells, cells), 0) == well_ref[...]
    ).astype(F32).astype(BF16)
    rates_t[...] = (
        0.5 * TIME_STEP * dot(rate_ref[...].astype(F32).T.astype(BF16), hot_well, 1, 0)
    ).astype(BF16)
    kt[...] = jnp.zeros_like(kt)
    gram[...] = jnp.zeros_like(gram)
    hot_own[...] = (
        lax.broadcasted_iota(jnp.int32, (profiles, block), 0) == prof_ref[me]
    ).astype(F32).T.astype(BF16)
    for copy in loads:
        copy.wait()

    per = devices // CHUNKS

    def build(c):
        s = sched[:, part(c, sub), :].reshape(full, n)
        half = dot(s, mix[...], 1, 1)
        state = (half * ((1.0 + TIME_STEP) - (4.0 * TIME_STEP) * (half * half))).astype(BF16)
        tile[c] = state
        kt[...] += dot(s.astype(F32).T.astype(BF16), state, 1, 0)
        x[c] = dot(cell_t[...], state, 1, 1).T.astype(BF16)
        for g in range(per):
            p = c * per + g
            owner = (p % depth) * 4 + ((p // depth) % 2) * 2 + p // (2 * depth)
            rows = sched[p]
            hot = (
                lax.broadcasted_iota(jnp.int32, (profiles, block), 0) == prof_ref[owner]
            ).astype(F32).astype(BF16)
            both = jnp.concatenate([rows.astype(F32).T.astype(BF16), hot], axis=0)
            gram[...] += dot(both, rows, 1, 0)

    def ahead(c, carry):
        build(c)
        return carry

    lax.fori_loop(0, AHEAD, ahead, 0)
    pl.semaphore_wait(barrier, chips)
    for c in range(AHEAD):
        hop0(c).start()
    reduce_start(
        "c", [dot(cell_t[...], cell_ref[...], 1, 0), dot(rates_t[...], cell_ref[...], 1, 0)]
    )
    for c in range(AHEAD - 1):
        fold0(c)

    def phase(c, carry):
        build(c)
        hop0(c).start()
        fold0(c - 1)
        pl.when(c == AHEAD)(lambda: reduce_chips("c"))
        pl.when(c == AHEAD + 2)(lambda: reduce_share("c"))
        pl.when(c == AHEAD + 4)(lambda: reduce_mate("c"))
        pl.when(c >= LAG1)(lambda: fold1(c - LAG1))
        pl.when(c >= LAG2)(lambda: fold2(c - LAG2, l_acc, c - LAG2))
        return carry

    lax.fori_loop(AHEAD, CHUNKS, phase, 0)

    high, low = halves(gram[n:].T)
    k_t = (kt[...] + dot(high, rates_t[...], 1, 0) + dot(low, rates_t[...], 1, 0)) * (
        2.0 * PANEL_SCALE / n_sched
    )
    k = k_t.T
    k_ref[...] = k
    k_low[...] = k.astype(BF16)
    fold0(CHUNKS - 1)
    both = jnp.concatenate([cell_t[...].astype(F32), k_t], axis=0)
    reduce_start("g", [dot3(both, k_t, 1, 1), dot(rates_t[...], k_low[...], 1, 0)])

    def project(c, *blocks):
        y = dot(tile[c], k_low[...], 1, 0)
        for b in blocks:
            eliminate([wu, wv], b, BLOCK, exact)
        x[CHUNKS + c] = y.astype(BF16)
        hop0(CHUNKS + c).start()

    def add_hot(acc, table):
        high, low = halves(table)
        both = dot(hot_own[...], jnp.concatenate([high, low], axis=1), 1, 0)
        return acc + both[:, 0:n] + both[:, n:]

    def y_fold1(c):
        fold1(CHUNKS + c)

    def y_fold2(c):
        fold2(CHUNKS + c, y_acc, c)

    def l_fold2(c):
        fold2(c, l_acc, c)

    reduce_done("c")
    load(wu, block_of("c", 0))
    load(wv, gram[0:n])
    pieces = n // BLOCK
    wide = n // WIDE
    ahead_of = [range(pieces * c // CHUNKS, pieces * (c + 1) // CHUNKS) for c in range(CHUNKS)]
    project(0, *ahead_of[0])
    fold1(CHUNKS - 3)
    l_fold2(2)
    project(1, *ahead_of[1])
    fold0(CHUNKS)
    reduce_chips("g")
    project(2, *ahead_of[2])
    fold0(CHUNKS + 1)
    fold1(CHUNKS - 2)
    l_fold2(3)
    project(3, *ahead_of[3])
    fold0(CHUNKS + 2)
    project(4, *ahead_of[4])
    fold0(CHUNKS + 3)
    fold1(CHUNKS - 1)
    l_fold2(4)
    project(5, *ahead_of[5])
    fold0(CHUNKS + 4)
    project(6, *ahead_of[6])
    fold0(CHUNKS + 5)
    l_fold2(5)
    y_fold1(0)
    project(7, *ahead_of[7])
    fold0(CHUNKS + 6)
    reduce_share("g")
    l_fold2(6)
    y_fold1(1)
    fold0(CHUNKS + 7)
    l_fold2(7)

    left = add_hot(l_acc[...], block_of("c", 1)) * (2.0 * PANEL_SCALE / n_cells)
    l_t[...] = left.T
    reduce_start("l", [dot3(l_t[...], l_t[...], 1, 1)])

    size_u = float(n_cells) ** 0.5
    size_v = float(n_sched) ** 0.5
    inv[0] = factor_inverse(wu)
    inv[3] = factor_inverse(wv)
    own = sched[(bit + 2 * core) * depth + z]
    y_fold1(2)
    reduce_mate("g")
    reduce_chips("l")
    rows_ref[:, 0:n] = dot2(own, inv[3] * size_v, 1, 1)
    y_fold1(3)
    y_fold2(0)
    reduce_done("g")
    ck = block_of("g", 0)
    kk = block_of("g", 1)

    def project_out(slot, side):
        a = dot3(inv[slot], side, 1, 0)
        inv[slot + 1] = dot3(a, inv[slot], 0, 0)
        return dot3(a, a, 0, 0)

    load(wu, kk - project_out(0, ck))
    overlap = project_out(3, ck.T * (n_sched / n_cells))
    l_perp[...] = l_t[...] - dot(inv[4], own.astype(F32), 1, 1, HIGH)
    y_fold1(4)
    y_fold2(1)
    for b in range(wide // 2):
        eliminate([wu], b, WIDE, dot3)
    reduce_share("l")
    y_fold1(5)
    y_fold2(2)
    for b in range(wide // 2, wide):
        eliminate([wu], b, WIDE, dot3)
    inv[2] = factor_inverse(wu)
    inv[1] = -dot(inv[2], inv[1], 1, 0, HIGH)
    y_fold1(6)
    y_fold2(3)
    y_fold2(4)
    y_fold1(7)
    reduce_mate("l")
    def y_step0():
        size = y_core.shape[0]
        return remote(y_part.at[part(1 - core, size)], y_core, y_s.at[0], y_r.at[0], mate)

    def y_step1(k):
        return remote(y_all.at[chip], y_all.at[chip], yb_s.at[k], yb_r.at[k], on_chip(k))

    def y_step2():
        mine = y_fin.at[part(core, y_core.shape[0])]
        return remote(mine, mine, y_s.at[1], y_r.at[1], mate)

    reduce_done("l")
    ll = l_fin[0:n]
    load(wv, ll - overlap)
    eliminate([wv], 0, WIDE, dot3)
    y_fold2(5)
    y_fold2(6)
    y_fold2(7)

    right = add_hot(y_acc[...], block_of("g", 2))
    moved = dot3(inv[2], 2.0 * right, 1, 1) + dot3(
        inv[1], l_t[...] * (n_cells / PANEL_SCALE), 1, 0
    )
    y_part[...] = dot3(moved, l_perp[...], 1, 1)
    y_step0().start()
    for b in range(1, wide):
        eliminate([wv], b, WIDE, dot3)
    y_step0().wait_recv()
    y_all[chip] = (y_part[part(core, y_core.shape[0])] + y_core[...]).astype(BF16)
    for k in range(1, chips):
        y_step1(k).start()
    u11, u21, u22, v11 = [inv[i] for i in range(4)]
    v22 = factor_inverse(wv)
    v21 = -dot(v22, inv[4], 1, 0, HIGH)
    rows_ref[:, n:] = dot3(l_perp[...].T, v22 * size_v, 1, 1)
    k_unscale = n_sched / PANEL_SCALE
    l_unscale = n_cells / PANEL_SCALE
    scale = n / (float(n_cells) * float(n_sched)) ** 0.5
    t11 = dot3(u11, ck * k_unscale, 1, 0)
    t12 = dot3(u11, ll * l_unscale, 1, 0)
    t21 = dot3(u21, ck * k_unscale, 1, 0) + dot3(u22, kk * k_unscale, 1, 0)
    core_ref[0:n, 0:n] = scale * dot3(t11, v11, 1, 1)
    core_ref[n:, 0:n] = scale * dot3(t21, v11, 1, 1)
    core_ref[0:n, n:] = scale * (dot(t11, v21, 1, 1, HIGH) + dot(t12, v22, 1, 1, HIGH))
    cells_ref[:, 0:n] = dot2(cell_ref[...], u11 * size_u, 1, 1)
    cells_ref[:, n:] = dot2(cell_ref[...], u21 * size_u, 1, 1) + dot3(
        k_ref[...], u22 * size_u, 1, 1
    )
    def drain(t, carry):
        hop0(t).wait_send()
        hop1(t).wait_send()
        for k in range(1, depth):
            hop2(t, k).wait_send()
        return carry

    lax.fori_loop(0, 2 * CHUNKS, drain, 0)
    for name in small:
        step0(name).wait_send()
        for k in range(1, chips):
            step1(name, k).wait_send()
            step2(name, k).wait_send()
        step3(name).wait_send()
    for k in range(1, chips):
        y_step1(k).wait_recv()
    total = y_all[0].astype(F32)
    for i in range(1, chips):
        total = total + y_all[i].astype(F32)
    y_fin[part(core, y_core.shape[0])] = total
    y_step2().start()
    y_step2().wait_recv()
    core_ref[n:, n:] = scale * dot(y_fin[...], v22, 1, 1, HIGH)

    y_step0().wait_send()
    for k in range(1, chips):
        y_step1(k).wait_send()
    y_step2().wait_send()


def hand_on(*refs):
    half = len(refs) // 2
    for source, target in zip(refs[:half], refs[half:]):
        target[...] = source[...]


def local(cell_factor, sched_factor, core_matrix, rate_table, cell_well, sched_profile):
    cells, n = cell_factor.shape
    n_sched = sched_factor.shape[0]
    devices = lax.axis_size("cell")
    n_cells = cells * devices
    block = n_sched // devices
    wells, profiles = rate_table.shape
    depth = devices // 4
    chips = devices // 2
    sub = block // CHUNKS
    full = devices * sub
    sds = jax.ShapeDtypeStruct
    vmem = pl.BlockSpec(memory_space=pltpu.VMEM)
    dma = pltpu.SemaphoreType.DMA
    both = 2 * CHUNKS

    def reduced(rows):
        size = padded(rows, devices)
        return [
            pltpu.VMEM((size, n), F32),
            pltpu.VMEM((size // 2, n), F32),
            pltpu.VMEM((size // 2, n), F32),
            pltpu.VMEM((chips, size // devices, n), F32),
            pltpu.VMEM((size, n), F32),
        ]

    outs = pl.pallas_call(
        functools.partial(comm_kernel, devices, n_cells, n_sched),
        in_specs=[pl.BlockSpec(memory_space=pltpu.HBM)] * 6,
        out_specs=[vmem] * 3,
        out_shape=[
            pltpu.VMEM((cells, 2 * n), F32),
            pltpu.VMEM((block, 2 * n), F32),
            pltpu.VMEM((2 * n, 2 * n), F32),
        ],
        scratch_shapes=[
            pltpu.VMEM((cells, n), BF16),
            pltpu.VMEM((n, n), F32),
            pltpu.VMEM((wells, profiles), BF16),
            pltpu.VMEM((1, cells), jnp.int32),
            pltpu.VMEM((devices, 1, block), jnp.int32),
            pltpu.VMEM((devices, block, n), BF16),
            pltpu.VMEM((CHUNKS, full, cells), BF16),
            pltpu.VMEM((cells, n), BF16),
            pltpu.VMEM((n, cells), BF16),
            pltpu.VMEM((profiles, cells), BF16),
            pltpu.VMEM((n, cells), F32),
            pltpu.VMEM((cells, n), F32),
            pltpu.VMEM((cells, n), BF16),
            pltpu.VMEM((n + profiles, n), F32),
            pltpu.VMEM((both, full, n), BF16),
            pltpu.VMEM((both, full // 2, n), BF16),
            pltpu.VMEM((both, full // 4, n), BF16),
            pltpu.VMEM((both, depth, sub, n), BF16),
            pltpu.VMEM((block, n), F32),
            pltpu.VMEM((block, n), F32),
            pltpu.VMEM((n, block), F32),
            pltpu.VMEM((n, block), F32),
            pltpu.VMEM((block, profiles), BF16),
            pltpu.VMEM((n, 2 * n), F32),
            pltpu.VMEM((n, 2 * n), F32),
            pltpu.VMEM((6, n, n), F32),
        ]
        + reduced(n + profiles)
        + reduced(2 * n + profiles)
        + reduced(n)
        + [
            pltpu.VMEM((n, n), F32),
            pltpu.VMEM((n // 2, n), F32),
            pltpu.VMEM((chips, n // 2, n), BF16),
            pltpu.VMEM((n, n), F32),
            dma((9,)),
            dma((both,)), dma((both,)), dma((both,)), dma((both,)),
            dma((both, depth)), dma((both, depth)),
        ]
        + [dma((2,)), dma((2,)), dma((2, chips)), dma((2, chips))] * 3
        + [dma((2,)), dma((2,)), dma((chips,)), dma((chips,))],
        compiler_params=pltpu.CompilerParams(
            collective_id=0, has_side_effects=True, vmem_limit_bytes=VMEM_LIMIT
        ),
    )(
        *(
            pltpu.with_memory_space_constraint(a, pltpu.HBM)
            for a in (
                cell_factor, core_matrix, rate_table, cell_well.reshape(1, cells),
                sched_factor.reshape(depth, 4, block, n),
                sched_profile.reshape(devices, 1, block),
            )
        )
    )
    return tuple(
        pl.pallas_call(
            hand_on,
            in_specs=[vmem] * 3,
            out_specs=[vmem] * 3,
            out_shape=[sds(o.shape, o.dtype) for o in outs],
            compiler_params=pltpu.CompilerParams(vmem_limit_bytes=HAND_LIMIT),
        )(*outs)
    )


def solution(mesh):
    return jax.shard_map(
        local,
        mesh=mesh,
        in_specs=(
            P(("group", "cell"), None),
            P("group", None),
            P("group", None),
            P(),
            P(("group", "cell")),
            P("group"),
        ),
        out_specs=(P(("group", "cell"), None), P(("group", "cell"), None), P("group", None)),
        check_vma=False,
    )
```
